512 devices in a mesh: tok: 32 (over x, z_lo), exp: 16 (over y, z_hi, core).
Axes of the slice: x: 4, y: 4, z: 16 (z_hi: 2, z_lo: 8; z = z_hi * 8 + z_lo), core: 2. Of those that a mesh axis runs over, the one named last changes fastest.
Arguments:
- tokens_x: bfloat16 [5120, 4096], P('tok', 'exp'), may hold values from -6 to 6
- out_grad: bfloat16 [5120, 4096], P('tok', 'exp'), may hold values from -12 to 12
- expert_ids: int32 [5120, 8], P('tok'), may hold values from 0 to 127, as said below
- route_q: int32 [5120, 8], P('tok'), may hold values from 1 to 255
- gate_w: bfloat16 [16, 1536, 4096], P('exp', 'tok'), may hold values from -0.09375 to 0.09375
- up_w: bfloat16 [16, 1536, 4096], P('exp', 'tok'), may hold values from -0.09375 to 0.09375
- down_w: bfloat16 [16, 1536, 4096], P('exp', 'tok'), may hold values from -0.15625 to 0.15625
Outputs:
- input_factor: float32 [16, 4096, 4096], P('exp', 'tok')
- grad_factor: float32 [16, 1536, 1536], P('exp', 'tok')
The draws below stay inside these ranges and needn't reach their ends.
Inputs may be any that keep to these rules, and one draw needn't show every extreme that they name: `expert_ids`: each token names exactly one expert from each range of 16 ids that starts at a multiple of 16, in varying positions of its row. Within the rows of one index of tok (aligned blocks of 160 rows) no expert below 16 is named by more than 20 rows, and in every draw one expert below 16 is named by exactly 20 rows in every block.
All inputs are finite; a program needn't handle non-finite values.
Results may differ from the reference program's by a relative error of at most 0.0056.
Values may be sent and summed in bfloat16 or wider, within the bound.
No kernel may reach another device: no remote copies, remote signals or barrier semaphores. Data moves between devices by JAX's collectives and lax.ppermute only.
A program may use at most 64 MiB of HBM per device.

```python
import jax
import jax.numpy as jnp
from jax import lax

D = 4096
FF = 1536
TOPK = 8
TOK_DEV = 160
TOKENS = 5120
CAP = 20
ROWS = 640
N_TOK = 32
N_EXP = 16


def rank_block(block_key):
    return jax.random.permutation(block_key, TOK_DEV)


def other_block(block_key):
    return jax.random.permutation(block_key, N_EXP - 1)


def draw_expert_ids(key, part):
    key_star, key_rank, key_other, key_rest, key_turn = jax.random.split(key, 5)
    blocks = TOKENS // TOK_DEV
    favored = jax.random.randint(key_star, (), 0, N_EXP)
    ranking = jax.vmap(rank_block)(jax.random.split(key_rank, blocks))
    others = jax.vmap(other_block)(jax.random.split(key_other, blocks))
    spill = jnp.maximum(ranking - CAP, 0) % (N_EXP - 1)
    other_ids = (favored + 1 + jnp.take_along_axis(others, spill, axis=1)) % N_EXP
    chosen = jnp.where(ranking < CAP, favored, other_ids).reshape(TOKENS)
    remaining = jax.random.randint(key_rest, (TOKENS, TOPK - 1), 0, N_EXP)
    offsets = jnp.arange(1, TOPK, dtype=jnp.int32) * N_EXP
    listed = jnp.concatenate([chosen[:, None], remaining + offsets[None, :]], axis=1)
    rotation = jax.random.randint(key_turn, (TOKENS, 1), 0, TOPK)
    ordering = (jnp.arange(TOPK, dtype=jnp.int32)[None, :] + rotation) % TOPK
    return jnp.take_along_axis(listed, ordering, axis=1).astype(jnp.int32)


def set_ends(entries, stream_key, low, top_value):
    longest = entries.shape.index(max(entries.shape))
    spots = []
    for shift in (0, 1):
        where = [jax.random.randint(jax.random.fold_in(stream_key, axis), (), 0, length) for axis, length in enumerate(entries.shape)]
        where[longest] = (where[longest] + shift) % entries.shape[longest]
        spots.append(tuple(where))
    return entries.at[spots[0]].set(low).at[spots[1]].set(top_value)


def shard_levels(own_key, shape, cuts, least, largest):
    factor_of = 1.0
    for axis_at, blocks in cuts:
        steps = jax.random.uniform(jax.random.fold_in(jax.random.fold_in(own_key, 6), axis_at), (blocks,), jnp.float32, least / len(cuts), largest / len(cuts))
        factor_of = factor_of * jnp.repeat(jnp.exp(steps), shape[axis_at] // blocks).reshape((-1,) + (1,) * (len(shape) - 1 - axis_at))
    return factor_of


def bell_draw(own_key, extent, spread, reach, shards=(), kind=jnp.bfloat16):
    array = spread * jax.random.normal(own_key, extent, jnp.float32)
    if shards:
        array = array * shard_levels(own_key, extent, shards, -0.22, 0.18)
    return jnp.clip(array, -reach, reach).astype(kind)


def setup_inputs(seed: int = 0) -> dict:
    splits = jax.random.split(jax.random.key(seed), 8)
    return {
        "tokens_x": bell_draw(splits[0], (TOKENS, D), 1.0, 6.0, ((0, 32), (1, 16))),
        "out_grad": bell_draw(splits[1], (TOKENS, D), 3.0, 12.0, ((0, 32), (1, 16))),
        "expert_ids": draw_expert_ids(jax.random.fold_in(splits[7], 71), 0),
        "route_q": set_ends(jax.random.randint(splits[3], (TOKENS, TOPK), 1, 256), jax.random.fold_in(splits[3], 1), 1, 255).astype(jnp.int32),
        "gate_w": bell_draw(splits[4], (N_EXP, FF, D), D ** -0.5, 0.09375, ((0, 16), (1, 32))),
        "up_w": bell_draw(splits[5], (N_EXP, FF, D), D ** -0.5, 0.09375, ((0, 16), (1, 32))),
        "down_w": bell_draw(splits[6], (N_EXP, FF, D), FF ** -0.5, 0.15625, ((0, 16), (1, 32))),
    }


def silu_slope(values):
    sigma = jax.nn.sigmoid(values)
    return sigma * (1.0 + values * (1.0 - sigma))


def reference(tokens_x, out_grad, expert_ids, route_q, gate_w, up_w, down_w):
    fitted = expert_ids < N_EXP
    fitted_id = jnp.sum(jnp.where(fitted, expert_ids, 0), axis=1).astype(jnp.int32)
    route_weight = jnp.sum(jnp.where(fitted, route_q, 0), axis=1).astype(jnp.float32) / 256.0
    onehot = (fitted_id[:, None] == jnp.arange(N_EXP, dtype=jnp.int32)[None, :]).astype(jnp.int32)
    running = jnp.cumsum(onehot.reshape(N_TOK, TOK_DEV, N_EXP), axis=1).astype(jnp.int32)
    running = running.reshape(TOKENS, N_EXP)
    rank_in = (jnp.sum(running * onehot, axis=1) - 1).astype(jnp.int32)
    shard_of = (jnp.arange(TOKENS, dtype=jnp.int32) // TOK_DEV).astype(jnp.int32)
    slot_ids = (fitted_id * ROWS + shard_of * CAP + rank_in).astype(jnp.int32)
    scaled_grad = (route_weight[:, None] * out_grad.astype(jnp.float32)).astype(jnp.bfloat16)
    x_slots = jnp.zeros((N_EXP * ROWS, D), jnp.bfloat16).at[slot_ids].set(tokens_x)
    g_slots = jnp.zeros((N_EXP * ROWS, D), jnp.bfloat16).at[slot_ids].set(scaled_grad)
    x_slots = x_slots.reshape(N_EXP, ROWS, D)
    g_slots = g_slots.reshape(N_EXP, ROWS, D)

    def per_expert(operand):
        x_rows, g_rows, w_gate, w_up, w_down = operand
        gate_pre = jnp.dot(x_rows, w_gate.T, preferred_element_type=jnp.float32)
        up_pre = jnp.dot(x_rows, w_up.T, preferred_element_type=jnp.float32)
        hidden_grad = jnp.dot(g_rows, w_down.T, preferred_element_type=jnp.float32)
        gate_grad = (hidden_grad * up_pre * silu_slope(gate_pre)).astype(jnp.bfloat16)
        in_factor = jnp.dot(x_rows.T, x_rows, preferred_element_type=jnp.float32) / ROWS
        grad_out = jnp.dot(gate_grad.T, gate_grad, preferred_element_type=jnp.float32) / ROWS
        return in_factor, grad_out

    input_factor, grad_factor = lax.map(per_expert, (x_slots, g_slots, gate_w, up_w, down_w))
    return (input_factor, grad_factor)
```

```python
import jax
import jax.numpy as jnp
from jax import lax
from jax.sharding import Mesh, PartitionSpec as P


F32 = jnp.float32
BF16 = jnp.bfloat16


def silu_slope(values):
    sigma = jax.nn.sigmoid(values)
    return sigma * (1.0 + values * (1.0 - sigma))


def dot_nt(a, b):
    return lax.dot_general(a, b, (((1,), (1,)), ((), ())), preferred_element_type=F32)


def dot_tn(a, b):
    return lax.dot_general(a, b, (((0,), (0,)), ((), ())), preferred_element_type=F32)


def local(tokens_x, out_grad, expert_ids, route_q, gate_w, up_w, down_w):
    nx = lax.axis_size("x")
    nz = lax.axis_size("zl")
    ny = lax.axis_size("y")
    owners = ny * lax.axis_size("zh") * lax.axis_size("c")
    xi = lax.axis_index("x")
    zi = lax.axis_index("zl")
    tok_rows, local_width = tokens_x.shape
    capacity = 2 * tok_rows // owners
    slot_count = capacity * nx * nz
    full_width = local_width * owners
    block = full_width // nx
    hid = gate_w.shape[1]

    def shift(v, s):
        return lax.ppermute(v, "x", [(i, (i + s) % nx) for i in range(nx)])

    fitted = expert_ids < owners
    fitted_id = jnp.sum(jnp.where(fitted, expert_ids, 0), axis=1)
    route_weight = jnp.sum(jnp.where(fitted, route_q, 0), axis=1).astype(F32) / 256.0
    onehot = (fitted_id[:, None] == jnp.arange(owners, dtype=jnp.int32)[None, :]).astype(jnp.int32)
    running = jnp.cumsum(onehot, axis=0)
    rank_in = jnp.sum(running * onehot, axis=1) - 1
    slot_ids = fitted_id * capacity + rank_in
    scaled = (route_weight[:, None] * out_grad.astype(F32)).astype(BF16)

    turn = [(i * ny + j, j * ny + i) for i in range(nx) for j in range(ny)]
    t_x = lax.ppermute(tokens_x, ("x", "y"), turn)
    t_g = lax.ppermute(scaled, ("x", "y"), turn)
    t_slot = lax.ppermute(slot_ids, ("x", "y"), turn)
    packer = (t_slot[None, :] == jnp.arange(owners * capacity, dtype=jnp.int32)[:, None]).astype(BF16)
    both = jnp.concatenate([t_x, t_g], axis=1)
    packed = jnp.dot(packer, both, preferred_element_type=F32).astype(BF16)
    packed = packed.reshape(owners, capacity, 2 * local_width)
    recv = lax.all_to_all(packed, ("y", "zh", "c"), split_axis=0, concat_axis=0, tiled=True)
    recv = recv.reshape(ny, owners // ny, capacity, 2, local_width)
    rows = ny * capacity
    own_x = recv[:, :, :, 0].transpose(0, 2, 1, 3).reshape(rows, block)
    own_g = recv[:, :, :, 1].transpose(0, 2, 1, 3).reshape(rows, block)

    def piece(s):
        start = ((xi + s) % nx) * block
        return jnp.concatenate(
            [lax.dynamic_slice_in_dim(w[0], start, block, 1) for w in (gate_w, up_w, down_w)], axis=0
        )

    weights = [piece(0)] + [shift(piece(s), s) for s in range(1, nx)]

    right_pairs = [(i, i + 1) for i in range(nz - 1)]
    left_pairs = [(i + 1, i) for i in range(nz - 1)]

    def ring(own):
        right, left = [own], [own]
        for _ in range(nz - 1):
            right.append(lax.ppermute(right[-1], "zl", right_pairs))
            left.append(lax.ppermute(left[-1], "zl", left_pairs))
        out = jnp.zeros((nz,) + own.shape, own.dtype)
        out = lax.dynamic_update_slice_in_dim(out, own[None], zi, 0)
        for k in range(1, nz):
            part = jnp.where(zi >= k, right[k], left[nz - k])
            out = lax.dynamic_update_slice_in_dim(out, part[None], (zi + nz - k) % nz, 0)
        return out.reshape(nz * own.shape[0], own.shape[1])

    x_all = ring(own_x)
    g_all = ring(own_g)

    def reduce_x(rel, moved):
        total = dot_nt(rel(weights[0]), moved)
        for s in range(1, nx):
            total = total + shift(dot_nt(rel(weights[s]), moved), -s)
        return total

    pre = reduce_x(lambda w: w[: 2 * hid], x_all)
    hidden_grad = reduce_x(lambda w: w[2 * hid :], g_all)
    gate_pre, up_pre = pre[:hid], pre[hid:]
    gate_grad = (hidden_grad * up_pre * silu_slope(gate_pre)).astype(BF16)

    strip_width = full_width // (nx * nz)
    strip = lax.dynamic_slice_in_dim(x_all, zi * strip_width, strip_width, 1)
    input_rows = jnp.zeros((strip_width, full_width), F32)
    for s in range(nx):
        theirs = strip if s == 0 else shift(strip, s)
        part = dot_tn(theirs, x_all) / float(slot_count)
        part = part if s == 0 else shift(part, -s)
        input_rows = lax.dynamic_update_slice_in_dim(input_rows, part, ((xi + s) % nx) * block, 1)

    held = gate_grad[None]
    bit = nz // 2
    while bit:
        other = lax.ppermute(held, "zl", [(i, i ^ bit) for i in range(nz)])
        low = (zi & bit) == 0
        held = jnp.stack([jnp.where(low, held, other), jnp.where(low, other, held)])
        held = held.reshape((-1,) + gate_grad.shape)
        bit //= 2
    levels = nz.bit_length() - 1
    held = held.reshape((2,) * levels + gate_grad.shape)
    held = held.transpose(tuple(range(levels))[::-1] + (levels, levels + 1))
    held = held.reshape(nz * hid, slot_count)
    grad_rows = jnp.zeros((hid, nx * nz * hid), F32)
    for s in range(nx):
        theirs = gate_grad if s == 0 else shift(gate_grad, s)
        part = dot_nt(theirs, held) / float(slot_count)
        part = part if s == 0 else shift(part, -s)
        grad_rows = lax.dynamic_update_slice_in_dim(grad_rows, part, ((xi + s) % nx) * nz * hid, 1)
    return (input_rows[None], grad_rows[None])


def solution(mesh):
    fine = Mesh(mesh.devices.reshape(4, 8, 4, 2, 2), ("x", "zl", "y", "zh", "c"))
    tok, exp = ("x", "zl"), ("y", "zh", "c")
    placed = (
        P(tok, exp),
        P(tok, exp),
        P(tok, None),
        P(tok, None),
        P(exp, tok, None),
        P(exp, tok, None),
        P(exp, tok, None),
    )
    return jax.shard_map(
        local,
        mesh=fine,
        in_specs=placed,
        out_specs=(P(exp, tok, None), P(exp, tok, None)),
        check_vma=False,
    )
```

```python
import jax
import jax.numpy as jnp
from jax import lax
from jax.sharding import Mesh, PartitionSpec as P


F32 = jnp.float32
BF16 = jnp.bfloat16


def silu_slope(values):
    sigma = jax.nn.sigmoid(values)
    return sigma * (1.0 + values * (1.0 - sigma))


def dot_nt(a, b):
    return lax.dot_general(a, b, (((1,), (1,)), ((), ())), preferred_element_type=F32)


def dot_tn(a, b):
    return lax.dot_general(a, b, (((0,), (0,)), ((), ())), preferred_element_type=F32)


def local(tokens_x, out_grad, expert_ids, route_q, gate_w, up_w, down_w):
    nx = lax.axis_size("x")
    nz = lax.axis_size("zl")
    owners = lax.axis_size("y") * lax.axis_size("zh") * lax.axis_size("c")
    xi = lax.axis_index("x")
    zi = lax.axis_index("zl")
    tok_rows, local_width = tokens_x.shape
    capacity = 2 * tok_rows // owners
    slot_count = capacity * nx * nz
    full_width = local_width * owners
    folds = 4
    hid = gate_w.shape[1]

    fitted = expert_ids < owners
    fitted_id = jnp.sum(jnp.where(fitted, expert_ids, 0), axis=1)
    route_weight = jnp.sum(jnp.where(fitted, route_q, 0), axis=1).astype(F32) / 256.0
    onehot = (fitted_id[:, None] == jnp.arange(owners, dtype=jnp.int32)[None, :]).astype(jnp.int32)
    running = jnp.cumsum(onehot, axis=0)
    rank_in = jnp.sum(running * onehot, axis=1) - 1
    slot_ids = fitted_id * capacity + rank_in
    scaled = (route_weight[:, None] * out_grad.astype(F32)).astype(BF16)
    packer = (slot_ids[None, :] == jnp.arange(owners * capacity, dtype=jnp.int32)[:, None]).astype(BF16)
    both = jnp.concatenate([tokens_x, scaled], axis=1)
    packed = jnp.dot(packer, both, preferred_element_type=F32).astype(BF16)
    packed = packed.reshape(owners, capacity, 2 * local_width)
    recv = lax.all_to_all(packed, ("y", "zh", "c"), split_axis=0, concat_axis=0, tiled=True)
    recv = recv.reshape(folds, owners // folds, capacity, 2, local_width)
    rows = folds * capacity
    cols = full_width // folds
    own_x = recv[:, :, :, 0].transpose(0, 2, 1, 3).reshape(rows, cols)
    own_g = recv[:, :, :, 1].transpose(0, 2, 1, 3).reshape(rows, cols)

    def swap_x(v, k):
        return lax.ppermute(v, "x", [(i, i ^ k) for i in range(nx)])

    zero = (recv[0, 0, 0, 0, :1] * 0).reshape(1, 1)
    w_up_half = jnp.concatenate([gate_w[0], up_w[0], down_w[0]], axis=0) + zero
    weights = [w_up_half] + [swap_x(w_up_half, k) for k in range(1, nx)]
    w_pre = jnp.concatenate([w[: 2 * hid] for w in weights], axis=0)
    w_down = jnp.concatenate([w[2 * hid :] for w in weights], axis=0)

    order = list(range(0, nz, 2)) + list(range(nz - 1, 0, -2))
    pairs = [(order[i], order[(i + 1) % nz]) for i in range(nz)]
    xs, gs = [own_x], [own_g]
    for _ in range(nz - 1):
        xs.append(lax.ppermute(xs[-1], "zl", pairs))
        gs.append(lax.ppermute(gs[-1], "zl", pairs))

    def unfold(parts):
        v = jnp.stack(parts).reshape(len(parts), folds, capacity, cols)
        return v.transpose(0, 2, 1, 3).reshape(len(parts) * capacity, full_width)

    half = nz // 2
    x_half = [unfold(xs[:half]), unfold(xs[half:])]
    x_rows = jnp.concatenate(x_half, axis=0)
    g_rows = jnp.concatenate([unfold(gs[:half]), unfold(gs[half:])], axis=0)

    slots = nz * capacity
    group = nx * hid
    pre = dot_nt(w_pre, x_rows).reshape(nx, 2, hid, slots)
    hidden_grad = dot_nt(w_down, g_rows).reshape(nx, hid, slots)
    gate_grad = hidden_grad * pre[:, 1] * silu_slope(pre[:, 0])
    gate_grad = gate_grad.astype(BF16).reshape(group, slots)

    place = jnp.where(zi % 2 == 0, zi // 2, nz - 1 - zi // 2)
    slot = jnp.arange(slots, dtype=jnp.int32)
    moved = ((place - slot // capacity + nz) % nz) * capacity + slot % capacity
    slot_perm = (moved[:, None] == slot[None, :]).astype(BF16)
    unit = jnp.arange(group, dtype=jnp.int32)
    from_unit = ((unit // hid) ^ xi) * hid + unit % hid
    unit_perm = (from_unit[None, :] == unit[:, None]).astype(BF16)
    g_sorted = jnp.dot(unit_perm, gate_grad, preferred_element_type=F32).astype(BF16)
    g_sorted = lax.dot_general(
        slot_perm, g_sorted, (((0,), (1,)), ((), ())), preferred_element_type=F32
    ).astype(BF16)

    wide = jnp.concatenate([g_sorted[: slots // 2], g_sorted[slots // 2 :]], axis=1)
    spread = jnp.broadcast_to(wide[None], (nz,) + wide.shape)
    spread = lax.all_to_all(spread, "zl", split_axis=0, concat_axis=0, tiled=True)
    spread = spread.reshape(nz, slots // 2, 2, nx, hid).transpose(2, 1, 3, 0, 4)
    spread = spread.reshape(slots, nx * nz * hid)
    part = dot_tn(g_sorted, spread).reshape(nx, hid, nx * nz * hid)
    part = lax.all_to_all(part, "x", split_axis=0, concat_axis=0, tiled=True)
    grad_rows = jnp.sum(part, axis=0) / float(slot_count)

    gathered = []
    for piece in x_half:
        gathered.append(piece)
        for k in range(1, nx):
            gathered.append(swap_x(piece, k))
    x_all = jnp.concatenate(gathered, axis=0)
    strip_width = full_width // (nx * nz)
    strip = lax.dynamic_slice_in_dim(x_all, (xi * nz + zi) * strip_width, strip_width, 1)
    input_rows = dot_tn(strip, x_all) / float(slot_count)
    return (input_rows[None], grad_rows[None])


def solution(mesh):
    fine = Mesh(mesh.devices.reshape(4, 8, 4, 2, 2), ("x", "zl", "y", "zh", "c"))
    tok, exp = ("x", "zl"), ("y", "zh", "c")
    placed = (
        P(tok, exp),
        P(tok, exp),
        P(tok, None),
        P(tok, None),
        P(exp, tok, None),
        P(exp, tok, None),
        P(exp, tok, None),
    )
    return jax.shard_map(
        local,
        mesh=fine,
        in_specs=placed,
        out_specs=(P(exp, tok, None), P(exp, tok, None)),
        check_vma=False,
    )
```

```python
import jax
import jax.numpy as jnp
from jax import lax
from jax.sharding import Mesh, PartitionSpec as P


F32 = jnp.float32
BF16 = jnp.bfloat16


def silu_slope(values):
    sigma = jax.nn.sigmoid(values)
    return sigma * (1.0 + values * (1.0 - sigma))


def dot_nt(a, b):
    return lax.dot_general(a, b, (((1,), (1,)), ((), ())), preferred_element_type=F32)


def dot_tn(a, b):
    return lax.dot_general(a, b, (((0,), (0,)), ((), ())), preferred_element_type=F32)


def body(tokens_x, out_grad, expert_ids, route_q, gate_w, up_w, down_w):
    nx = lax.axis_size("x")
    nz = lax.axis_size("zl")
    owners = lax.axis_size("y") * lax.axis_size("zh") * lax.axis_size("c")
    xi = lax.axis_index("x")
    zi = lax.axis_index("zl")
    tok_rows, local_width = tokens_x.shape
    capacity = 2 * tok_rows // owners
    slot_count = capacity * nx * nz
    full_width = local_width * owners
    hid = gate_w.shape[1]

    fitted = expert_ids < owners
    fitted_id = jnp.sum(jnp.where(fitted, expert_ids, 0), axis=1)
    route_weight = jnp.sum(jnp.where(fitted, route_q, 0), axis=1).astype(F32) / 256.0
    onehot = (fitted_id[:, None] == jnp.arange(owners, dtype=jnp.int32)[None, :]).astype(jnp.int32)
    running = jnp.cumsum(onehot, axis=0)
    rank_in = jnp.sum(running * onehot, axis=1) - 1
    row_ids = fitted_id * (2 * capacity) + rank_in
    scaled = (route_weight[:, None] * out_grad.astype(F32)).astype(BF16)
    both_ids = jnp.concatenate([row_ids, row_ids + capacity])
    packer = (both_ids[None, :] == jnp.arange(owners * 2 * capacity, dtype=jnp.int32)[:, None]).astype(BF16)
    both = jnp.concatenate([tokens_x, scaled], axis=0)
    packed = jnp.dot(packer, both, preferred_element_type=F32).astype(BF16)
    packed = packed.reshape(owners, 2 * capacity, local_width)
    recv = lax.all_to_all(packed, ("y", "zh", "c"), split_axis=0, concat_axis=0, tiled=True)
    own = recv.transpose(1, 0, 2).reshape(2 * capacity, full_width)

    def swap_x(v, k):
        return lax.ppermute(v, "x", [(i, i ^ k) for i in range(nx)])

    zero = (recv[0, :1, :1] * 0).reshape(1, 1)
    w_own = jnp.concatenate([gate_w[0], up_w[0], down_w[0]], axis=0) + zero
    weights = [w_own] + [swap_x(w_own, k) for k in range(1, nx)]

    order = list(range(0, nz, 2)) + list(range(nz - 1, 0, -2))
    pairs = [(order[i], order[(i + 1) % nz]) for i in range(nz)]
    parts = [own]
    for _ in range(1, nz):
        parts.append(lax.ppermute(parts[-1], "zl", pairs))

    half = nz // 2
    group = nx * hid
    slots = nz * capacity
    place = jnp.where(zi % 2 == 0, zi // 2, nz - 1 - zi // 2)
    unit = jnp.arange(group, dtype=jnp.int32)
    from_unit = ((unit // hid) ^ xi) * hid + unit % hid
    unit_perm = (from_unit[:, None] == unit[None, :]).astype(BF16)
    column = jnp.arange(half * 2 * capacity, dtype=jnp.int32)
    slot = jnp.arange(slots, dtype=jnp.int32)

    sorted_f32 = 0.0
    x_half = []
    for h in range(2):
        rows = jnp.concatenate(parts[h * half : (h + 1) * half], axis=0)
        x_half.append(
            rows.reshape(half, 2 * capacity, full_width)[:, :capacity].reshape(half * capacity, full_width)
        )
        pre = []
        for w in weights:
            pre.append(dot_nt(w, rows))
        pre = jnp.stack(pre)
        gate_pre, up_pre = pre[:, :hid], pre[:, hid : 2 * hid]
        hidden_grad = jnp.roll(pre[:, 2 * hid :], -capacity, axis=2)
        gate_grad = (hidden_grad * up_pre * silu_slope(gate_pre)).astype(BF16).reshape(group, -1)
        arrival = h * half + column // (2 * capacity)
        within = column % (2 * capacity)
        target = jnp.where(within < capacity, ((place - arrival + nz) % nz) * capacity + within, -1)
        slot_perm = (slot[:, None] == target[None, :]).astype(BF16)
        sorted_f32 = sorted_f32 + dot_nt(slot_perm, gate_grad)
    g_sorted = jnp.dot(sorted_f32.astype(BF16), unit_perm, preferred_element_type=F32).astype(BF16)

    wide = jnp.concatenate([g_sorted[: slots // 2], g_sorted[slots // 2 :]], axis=1)
    spread = jnp.broadcast_to(wide[None], (nz,) + wide.shape)
    spread = lax.all_to_all(spread, "zl", split_axis=0, concat_axis=0, tiled=True)
    spread = spread.reshape(nz, slots // 2, 2, nx, hid).transpose(2, 1, 3, 0, 4)
    spread = spread.reshape(slots, nx * nz * hid)
    part_sent = dot_tn(g_sorted, spread).astype(BF16).reshape(nx, hid, nx * nz * hid)
    part = lax.all_to_all(part_sent, "x", split_axis=0, concat_axis=0, tiled=True)
    grad_rows = jnp.sum(part.astype(F32), axis=0) / float(slot_count)

    strip_width = full_width // (nx * nz)
    late = (part_sent[0, :1, :1] * 0).reshape(1, 1)
    input_rows = 0.0
    for name, piece in zip(("xa", "xb"), x_half):
        own_piece = piece if name == "xa" else piece + late
        gathered = [own_piece] + [swap_x(piece, k) for k in range(1, nx)]
        rows = jnp.concatenate(gathered, axis=0)
        strip = lax.dynamic_slice_in_dim(rows, (xi * nz + zi) * strip_width, strip_width, 1)
        input_rows = input_rows + dot_tn(strip, rows) / float(slot_count)
    return (input_rows[None], grad_rows[None])


def solution(mesh):
    fine = Mesh(mesh.devices.reshape(4, 8, 4, 2, 2), ("x", "zl", "y", "zh", "c"))
    tok, exp = ("x", "zl"), ("y", "zh", "c")
    placed = (
        P(tok, exp),
        P(tok, exp),
        P(tok, None),
        P(tok, None),
        P(exp, tok, None),
        P(exp, tok, None),
        P(exp, tok, None),
    )
    return jax.shard_map(
        body,
        mesh=fine,
        in_specs=placed,
        out_specs=(P(exp, tok, None), P(exp, tok, None)),
        check_vma=False,
    )
```

```python
import jax
import jax.numpy as jnp
from jax import lax
from jax.sharding import Mesh, PartitionSpec as P


F32 = jnp.float32
BF16 = jnp.bfloat16


def silu_slope(values):
    sigma = jax.nn.sigmoid(values)
    return sigma * (1.0 + values * (1.0 - sigma))


def dot_nt(a, b):
    return lax.dot_general(a, b, (((1,), (1,)), ((), ())), preferred_element_type=F32)


def dot_tn(a, b):
    return lax.dot_general(a, b, (((0,), (0,)), ((), ())), preferred_element_type=F32)


def body(tokens_x, out_grad, expert_ids, route_q, gate_w, up_w, down_w):
    nx = lax.axis_size("x")
    nz = lax.axis_size("zl")
    owners = lax.axis_size("y") * lax.axis_size("zh") * lax.axis_size("c")
    xi = lax.axis_index("x")
    zi = lax.axis_index("zl")
    tok_rows, local_width = tokens_x.shape
    capacity = 2 * tok_rows // owners
    slot_count = capacity * nx * nz
    full_width = local_width * owners
    hid = gate_w.shape[1]

    fitted = expert_ids < owners
    fitted_id = jnp.sum(jnp.where(fitted, expert_ids, 0), axis=1)
    route_weight = jnp.sum(jnp.where(fitted, route_q, 0), axis=1).astype(F32) / 256.0
    onehot = (fitted_id[:, None] == jnp.arange(owners, dtype=jnp.int32)[None, :]).astype(jnp.int32)
    running = jnp.cumsum(onehot, axis=0)
    rank_in = jnp.sum(running * onehot, axis=1) - 1
    row_ids = fitted_id * (2 * capacity) + rank_in
    scaled = (route_weight[:, None] * out_grad.astype(F32)).astype(BF16)
    both_ids = jnp.concatenate([row_ids, row_ids + capacity])
    packer = (both_ids[None, :] == jnp.arange(owners * 2 * capacity, dtype=jnp.int32)[:, None]).astype(BF16)
    both = jnp.concatenate([tokens_x, scaled], axis=0)
    packed = jnp.dot(packer, both, preferred_element_type=F32).astype(BF16)
    packed = packed.reshape(owners, 2 * capacity, local_width)
    recv = lax.all_to_all(packed, ("y", "zh", "c"), split_axis=0, concat_axis=0, tiled=True)
    own = recv.transpose(1, 0, 2).reshape(2 * capacity, full_width)

    def swap_x(v, k):
        return lax.ppermute(v, "x", [(i, i ^ k) for i in range(nx)])

    w_own = jnp.concatenate([gate_w[0], up_w[0], down_w[0]], axis=0)
    w_others = [swap_x(w_own, k) for k in range(1, nx)]

    order = list(range(0, nz, 2)) + list(range(nz - 1, 0, -2))
    pairs = [(order[i], order[(i + 1) % nz]) for i in range(nz)]
    parts = [own]
    for _ in range(1, nz):
        parts.append(lax.ppermute(parts[-1], "zl", pairs))

    half = nz // 2

    late = [(parts[half + i][:1, :1] * 0).reshape(1, 1) for i in range(2)]
    stacked = [w_own, w_others[0] + late[0], w_others[1] + late[1]] + w_others[2:]
    weights = jnp.concatenate(stacked, axis=0)

    group = nx * hid
    slots = nz * capacity
    place = jnp.where(zi % 2 == 0, zi // 2, nz - 1 - zi // 2)
    unit = jnp.arange(group, dtype=jnp.int32)
    from_unit = ((unit // hid) ^ xi) * hid + unit % hid
    unit_perm = (from_unit[:, None] == unit[None, :]).astype(BF16)
    column = jnp.arange(half * 2 * capacity, dtype=jnp.int32)
    slot = jnp.arange(slots, dtype=jnp.int32)

    sorted_f32 = 0.0
    x_half = []
    for h in range(2):
        rows = jnp.concatenate(parts[h * half : (h + 1) * half], axis=0)
        x_half.append(
            rows.reshape(half, 2 * capacity, full_width)[:, :capacity].reshape(half * capacity, full_width)
        )
        pre = dot_nt(weights, rows).reshape(nx, 3 * hid, -1)
        gate_pre, up_pre = pre[:, :hid], pre[:, hid : 2 * hid]
        hidden_grad = jnp.roll(pre[:, 2 * hid :], -capacity, axis=2)
        gate_grad = (hidden_grad * up_pre * silu_slope(gate_pre)).astype(BF16).reshape(group, -1)
        arrival = h * half + column // (2 * capacity)
        within = column % (2 * capacity)
        target = jnp.where(within < capacity, ((place - arrival + nz) % nz) * capacity + within, -1)
        slot_perm = (slot[:, None] == target[None, :]).astype(BF16)
        sorted_f32 = sorted_f32 + dot_nt(slot_perm, gate_grad)
    g_sorted = jnp.dot(sorted_f32.astype(BF16), unit_perm, preferred_element_type=F32).astype(BF16)

    wide = jnp.concatenate([g_sorted[: slots // 2], g_sorted[slots // 2 :]], axis=1)
    spread = jnp.broadcast_to(wide[None], (nz,) + wide.shape)
    spread = lax.all_to_all(spread, "zl", split_axis=0, concat_axis=0, tiled=True)
    later = (spread[0, :1, :1] * 0).reshape(1, 1)
    spread = spread.reshape(nz, slots // 2, 2, nx, hid).transpose(2, 1, 3, 0, 4)
    spread = spread.reshape(slots, nx * nz * hid)
    part_sent = dot_tn(g_sorted, spread).astype(BF16).reshape(nx, hid, nx * nz * hid)
    part = lax.all_to_all(part_sent, "x", split_axis=0, concat_axis=0, tiled=True)
    grad_rows = jnp.sum(part.astype(F32), axis=0) / float(slot_count)

    strip_width = full_width // (nx * nz)
    input_rows = 0.0
    for name, piece in zip(("xa", "xb"), x_half):
        own_piece = piece if name == "xa" else piece + later
        gathered = [own_piece] + [swap_x(piece, k) for k in range(1, nx)]
        rows = jnp.concatenate(gathered, axis=0)
        strip = lax.dynamic_slice_in_dim(rows, (xi * nz + zi) * strip_width, strip_width, 1)
        input_rows = input_rows + dot_tn(strip, rows) / float(slot_count)
    return (input_rows[None], grad_rows[None])


def solution(mesh):
    fine = Mesh(mesh.devices.reshape(4, 8, 4, 2, 2), ("x", "zl", "y", "zh", "c"))
    tok, exp = ("x", "zl"), ("y", "zh", "c")
    placed = (
        P(tok, exp),
        P(tok, exp),
        P(tok, None),
        P(tok, None),
        P(exp, tok, None),
        P(exp, tok, None),
        P(exp, tok, None),
    )
    return jax.shard_map(
        body,
        mesh=fine,
        in_specs=placed,
        out_specs=(P(exp, tok, None), P(exp, tok, None)),
        check_vma=False,
    )
```

```python
import jax
import jax.numpy as jnp
from jax import lax
from jax.sharding import Mesh, PartitionSpec as P


F32 = jnp.float32
BF16 = jnp.bfloat16


def silu_slope(values):
    sigma = jax.nn.sigmoid(values)
    return sigma * (1.0 + values * (1.0 - sigma))


def dot_nt(a, b):
    return lax.dot_general(a, b, (((1,), (1,)), ((), ())), preferred_element_type=F32)


def dot_tn(a, b):
    return lax.dot_general(a, b, (((0,), (0,)), ((), ())), preferred_element_type=F32)


def body(tokens_x, out_grad, expert_ids, route_q, gate_w, up_w, down_w):
    nx = lax.axis_size("x")
    nz = lax.axis_size("zl")
    owners = lax.axis_size("y") * lax.axis_size("zh") * lax.axis_size("c")
    xi = lax.axis_index("x")
    zi = lax.axis_index("zl")
    tok_rows, local_width = tokens_x.shape
    capacity = 2 * tok_rows // owners
    slot_count = capacity * nx * nz
    full_width = local_width * owners
    hid = gate_w.shape[1]

    fitted = expert_ids < owners
    fitted_id = jnp.sum(jnp.where(fitted, expert_ids, 0), axis=1)
    route_weight = jnp.sum(jnp.where(fitted, route_q, 0), axis=1).astype(F32) / 256.0
    onehot = (fitted_id[:, None] == jnp.arange(owners, dtype=jnp.int32)[None, :]).astype(jnp.int32)
    running = jnp.cumsum(onehot, axis=0)
    rank_in = jnp.sum(running * onehot, axis=1) - 1
    row_ids = fitted_id * (2 * capacity) + rank_in
    scaled = (route_weight[:, None] * out_grad.astype(F32)).astype(BF16)
    both_ids = jnp.concatenate([row_ids, row_ids + capacity])
    packer = (both_ids[None, :] == jnp.arange(owners * 2 * capacity, dtype=jnp.int32)[:, None]).astype(BF16)
    both = jnp.concatenate([tokens_x, scaled], axis=0)
    packed = jnp.dot(packer, both, preferred_element_type=F32).astype(BF16)
    packed = packed.reshape(owners, 2 * capacity, local_width)
    recv = lax.all_to_all(packed, ("y", "zh", "c"), split_axis=0, concat_axis=0, tiled=True)
    own = recv.transpose(1, 0, 2).reshape(2 * capacity, full_width)

    def swap_x(v, k):
        return lax.ppermute(v, "x", [(i, i ^ k) for i in range(nx)])

    w_own = jnp.concatenate([gate_w[0], up_w[0], down_w[0]], axis=0)
    w_others = [swap_x(w_own, k) for k in range(1, nx)]

    order = list(range(0, nz, 2)) + list(range(nz - 1, 0, -2))
    pairs = [(order[i], order[(i + 1) % nz]) for i in range(nz)]
    parts = [own]
    for _ in range(1, nz):
        parts.append(lax.ppermute(parts[-1], "zl", pairs))

    half = nz // 2

    late = [(parts[i][:1, :1] * 0).reshape(1, 1) for i in (2, 4)]
    weights = jnp.concatenate([w_own, w_others[0] + late[0], w_others[2], w_others[1] + late[1]], axis=0)

    group = nx * hid
    slots = nz * capacity
    place = jnp.where(zi % 2 == 0, zi // 2, nz - 1 - zi // 2)
    unit = jnp.arange(group, dtype=jnp.int32)
    offset = (unit // hid) ^ xi
    from_unit = (offset ^ (offset >> 1)) * hid + unit % hid
    unit_perm = (from_unit[:, None] == unit[None, :]).astype(BF16)
    column = jnp.arange(half * 2 * capacity, dtype=jnp.int32)
    lanes = 128
    rest = slots - lanes
    packed_col = jnp.arange((nx + 1) * lanes, dtype=jnp.int32)
    lane, part_of = packed_col % lanes, packed_col // lanes - 1
    slot = jnp.where(part_of < 0, lane, jnp.where(lane // rest == part_of, lanes + lane % rest, -2))

    sorted_f32 = 0.0
    x_half = []
    for h in range(2):
        rows = jnp.concatenate(parts[h * half : (h + 1) * half], axis=0)
        x_half.append(
            rows.reshape(half, 2 * capacity, full_width)[:, :capacity].reshape(half * capacity, full_width)
        )
        pre = dot_nt(weights, rows).reshape(nx, 3 * hid, -1)
        gate_pre, up_pre = pre[:, :hid], pre[:, hid : 2 * hid]
        hidden_grad = jnp.roll(pre[:, 2 * hid :], -capacity, axis=2)
        gate_grad = (hidden_grad * up_pre * silu_slope(gate_pre)).astype(BF16).reshape(group, -1)
        arrival = h * half + column // (2 * capacity)
        within = column % (2 * capacity)
        target = jnp.where(within < capacity, ((place - arrival + nz) % nz) * capacity + within, -1)
        slot_perm = (target[:, None] == slot[None, :]).astype(BF16)
        sorted_f32 = sorted_f32 + jnp.dot(gate_grad, slot_perm, preferred_element_type=F32)
    g_packed = jnp.dot(unit_perm, sorted_f32.astype(BF16), preferred_element_type=F32).astype(BF16)

    first = g_packed[:, :lanes]
    lasts = [g_packed[:, (1 + j) * lanes : (2 + j) * lanes] for j in range(nx)]
    tail = sum(v[j * hid : (j + 1) * hid] for j, v in enumerate(lasts))
    sent = jnp.concatenate([first, tail], axis=0)
    spread = jnp.broadcast_to(sent[None], (nz,) + sent.shape)
    spread = lax.all_to_all(spread, "zl", split_axis=0, concat_axis=0, tiled=True)
    later = (spread[0, :1, :1] * 0).reshape(1, 1)
    tails = spread[:, group:].reshape(nz * hid, lanes)
    cols = []
    for j in range(nx):
        theirs = spread[:, j * hid : (j + 1) * hid].reshape(nz * hid, lanes)
        both_j = jnp.concatenate([theirs, tails], axis=1)
        cols.append(dot_nt(jnp.concatenate([first, lasts[j]], axis=1), both_j).astype(BF16))
    part_sent = jnp.concatenate(cols, axis=1).reshape(nx, hid, nx * nz * hid)
    part = lax.all_to_all(part_sent, "x", split_axis=0, concat_axis=0, tiled=True)
    grad_rows = jnp.sum(part.astype(F32), axis=0) / float(slot_count)

    strip_width = full_width // (nx * nz)
    input_rows = 0.0
    for name, piece in zip(("xa", "xb"), x_half):
        own_piece = piece + (later if name == "xb" else (sent[:1, :1] * 0))
        gathered = [own_piece] + [swap_x(piece, k) for k in range(1, nx)]
        rows = jnp.concatenate(gathered, axis=0)
        strip = lax.dynamic_slice_in_dim(rows, (xi * nz + zi) * strip_width, strip_width, 1)
        input_rows = input_rows + dot_tn(strip, rows) / float(slot_count)
    return (input_rows[None], grad_rows[None])


def solution(mesh):
    fine = Mesh(mesh.devices.reshape(4, 8, 4, 2, 2), ("x", "zl", "y", "zh", "c"))
    tok, exp = ("x", "zl"), ("y", "zh", "c")
    placed = (
        P(tok, exp),
        P(tok, exp),
        P(tok, None),
        P(tok, None),
        P(exp, tok, None),
        P(exp, tok, None),
        P(exp, tok, None),
    )
    return jax.shard_map(
        body,
        mesh=fine,
        in_specs=placed,
        out_specs=(P(exp, tok, None), P(exp, tok, None)),
        check_vma=False,
    )
```

```python
import jax
import jax.numpy as jnp
from jax import lax
from jax.sharding import Mesh, PartitionSpec as P


F32 = jnp.float32
BF16 = jnp.bfloat16


def silu_slope(values):
    sigma = jax.nn.sigmoid(values)
    return sigma * (1.0 + values * (1.0 - sigma))


def dot_nt(a, b):
    return lax.dot_general(a, b, (((1,), (1,)), ((), ())), preferred_element_type=F32)


def dot_tn(a, b):
    return lax.dot_general(a, b, (((0,), (0,)), ((), ())), preferred_element_type=F32)


def body(tokens_x, out_grad, expert_ids, route_q, gate_w, up_w, down_w):
    nx = lax.axis_size("x")
    nz = lax.axis_size("zl")
    owners = lax.axis_size("y") * lax.axis_size("zh") * lax.axis_size("c")
    xi = lax.axis_index("x")
    zi = lax.axis_index("zl")
    tok_rows, local_width = tokens_x.shape
    capacity = 2 * tok_rows // owners
    slot_count = capacity * nx * nz
    full_width = local_width * owners
    hid = gate_w.shape[1]

    fitted = expert_ids < owners
    fitted_id = jnp.sum(jnp.where(fitted, expert_ids, 0), axis=1)
    route_weight = jnp.sum(jnp.where(fitted, route_q, 0), axis=1).astype(F32) / 256.0
    onehot = (fitted_id[:, None] == jnp.arange(owners, dtype=jnp.int32)[None, :]).astype(jnp.int32)
    running = jnp.cumsum(onehot, axis=0)
    rank_in = jnp.sum(running * onehot, axis=1) - 1
    row_ids = fitted_id * (2 * capacity) + rank_in
    scaled = (route_weight[:, None] * out_grad.astype(F32)).astype(BF16)
    both_ids = jnp.concatenate([row_ids, row_ids + capacity])
    packer = (both_ids[None, :] == jnp.arange(owners * 2 * capacity, dtype=jnp.int32)[:, None]).astype(BF16)
    both = jnp.concatenate([tokens_x, scaled], axis=0)
    packed = jnp.dot(packer, both, preferred_element_type=F32).astype(BF16)
    packed = packed.reshape(owners, 2 * capacity, local_width)
    recv = lax.all_to_all(packed, ("y", "zh", "c"), split_axis=0, concat_axis=0, tiled=True)
    own = recv.transpose(1, 0, 2).reshape(2 * capacity, full_width)

    def swap_x(v, k):
        return lax.ppermute(v, "x", [(i, i ^ k) for i in range(nx)])

    w_own = jnp.concatenate([gate_w[0], up_w[0], down_w[0]], axis=0)
    w_others = [swap_x(w_own, k) for k in range(1, nx)]

    order = list(range(0, nz, 2)) + list(range(nz - 1, 0, -2))
    pairs = [(order[i], order[(i + 1) % nz]) for i in range(nz)]
    back = [(j, i) for i, j in pairs]

    def hop(v, way):
        return lax.ppermute(v, "zl", way)

    fore, aft = [own], [own]
    for _ in range(1, nz // 2):
        fore.append(hop(fore[-1], pairs))
        aft.append(hop(aft[-1], back))
    mid = full_width // 2
    far = [hop(fore[-1][:, :mid], pairs), hop(aft[-1][:, mid:], back)]
    parts, steps = [own], [0]
    for k in range(1, nz // 2):
        parts += [fore[k], aft[k]]
        steps += [k, nz - k]
    parts.append(jnp.concatenate(far, axis=1))
    steps.append(nz // 2)
    half = nz // 2

    late = [(parts[i][:1, :1] * 0).reshape(1, 1) for i in (2, 4)]
    weights = jnp.concatenate([w_own, w_others[0] + late[0], w_others[2], w_others[1] + late[1]], axis=0)

    group = nx * hid
    slots = nz * capacity
    place = jnp.where(zi % 2 == 0, zi // 2, nz - 1 - zi // 2)
    unit = jnp.arange(group, dtype=jnp.int32)
    offset = (unit // hid) ^ xi
    from_unit = (offset ^ (offset >> 1)) * hid + unit % hid
    unit_perm = (from_unit[:, None] == unit[None, :]).astype(BF16)
    column = jnp.arange(half * 2 * capacity, dtype=jnp.int32)
    lanes = 128
    rest = slots - lanes
    packed_col = jnp.arange((nx + 1) * lanes, dtype=jnp.int32)
    lane, part_of = packed_col % lanes, packed_col // lanes - 1
    slot = jnp.where(part_of < 0, lane, jnp.where(lane // rest == part_of, lanes + lane % rest, -2))

    sorted_f32 = 0.0
    x_half = []
    for h in range(2):
        rows = jnp.concatenate(parts[h * half : (h + 1) * half], axis=0)
        x_rows = rows.reshape(half, 2 * capacity, full_width)[:, :capacity]
        x_half.append(x_rows.reshape(half * capacity, full_width))
        pre = dot_nt(weights, rows).reshape(nx, 3 * hid, -1)
        gate_pre, up_pre = pre[:, :hid], pre[:, hid : 2 * hid]
        hidden_grad = jnp.roll(pre[:, 2 * hid :], -capacity, axis=2)
        gate_grad = (hidden_grad * up_pre * silu_slope(gate_pre)).astype(BF16).reshape(group, -1)
        went = jnp.repeat(jnp.array(steps[h * half : (h + 1) * half], jnp.int32), 2 * capacity)
        within = column % (2 * capacity)
        target = jnp.where(within < capacity, ((place - went + nz) % nz) * capacity + within, -1)
        slot_perm = (target[:, None] == slot[None, :]).astype(BF16)
        sorted_f32 = sorted_f32 + jnp.dot(gate_grad, slot_perm, preferred_element_type=F32)
    g_packed = jnp.dot(unit_perm, sorted_f32.astype(BF16), preferred_element_type=F32).astype(BF16)

    first = g_packed[:, :lanes]
    lasts = [g_packed[:, (1 + j) * lanes : (2 + j) * lanes] for j in range(nx)]
    tail = sum(v[j * hid : (j + 1) * hid] for j, v in enumerate(lasts))
    sent = jnp.concatenate([first, tail], axis=0)
    spread = jnp.broadcast_to(sent[None], (nz,) + sent.shape)
    spread = lax.all_to_all(spread, "zl", split_axis=0, concat_axis=0, tiled=True)
    later = (spread[0, :1, :1] * 0).reshape(1, 1)
    tails = spread[:, group:].reshape(nz * hid, lanes)
    cols = []
    for j in range(nx):
        theirs = spread[:, j * hid : (j + 1) * hid].reshape(nz * hid, lanes)
        both_j = jnp.concatenate([theirs, tails], axis=1)
        sums = dot_nt(jnp.concatenate([first, lasts[j]], axis=1), both_j) / float(slot_count)
        cols.append(sums.astype(BF16))
    part_sent = jnp.concatenate(cols, axis=1).reshape(nx, hid, nx * nz * hid)
    part = lax.all_to_all(part_sent, "x", split_axis=0, concat_axis=0, tiled=True)
    grad_rows = jnp.sum(part.astype(F32), axis=0)

    strip_width = full_width // (nx * nz)
    input_rows = 0.0
    for name, piece in zip(("xa", "xb"), x_half):
        own_piece = piece + (later if name == "xb" else (sent[:1, :1] * 0))
        gathered = [own_piece] + [swap_x(piece, k) for k in range(1, nx)]
        rows = jnp.concatenate(gathered, axis=0)
        strip = lax.dynamic_slice_in_dim(rows, (xi * nz + zi) * strip_width, strip_width, 1)
        input_rows = input_rows + dot_tn(strip, rows) / float(slot_count)
    return (input_rows[None], grad_rows[None])


def solution(mesh):
    fine = Mesh(mesh.devices.reshape(4, 8, 4, 2, 2), ("x", "zl", "y", "zh", "c"))
    tok, exp = ("x", "zl"), ("y", "zh", "c")
    placed = (
        P(tok, exp),
        P(tok, exp),
        P(tok, None),
        P(tok, None),
        P(exp, tok, None),
        P(exp, tok, None),
        P(exp, tok, None),
    )
    return jax.shard_map(
        body,
        mesh=fine,
        in_specs=placed,
        out_specs=(P(exp, tok, None), P(exp, tok, None)),
        check_vma=False,
    )
```

```python
import jax
import jax.numpy as jnp
from jax import lax
from jax.sharding import Mesh, PartitionSpec as P


F32 = jnp.float32
BF16 = jnp.bfloat16


def silu_slope(values):
    sigma = jax.nn.sigmoid(values)
    return sigma * (1.0 + values * (1.0 - sigma))


def dot_nt(a, b):
    return lax.dot_general(a, b, (((1,), (1,)), ((), ())), preferred_element_type=F32)


def dot_tn(a, b):
    return lax.dot_general(a, b, (((0,), (0,)), ((), ())), preferred_element_type=F32)


def body(tokens_x, out_grad, expert_ids, route_q, gate_w, up_w, down_w):
    nx = lax.axis_size("x")
    nz = lax.axis_size("zl")
    owners = lax.axis_size("y") * lax.axis_size("zh") * lax.axis_size("c")
    xi = lax.axis_index("x")
    zi = lax.axis_index("zl")
    tok_rows, local_width = tokens_x.shape
    capacity = 2 * tok_rows // owners
    slot_count = capacity * nx * nz
    full_width = local_width * owners
    hid = gate_w.shape[1]

    fitted = expert_ids < owners
    fitted_id = jnp.sum(jnp.where(fitted, expert_ids, 0), axis=1)
    route_weight = jnp.sum(jnp.where(fitted, route_q, 0), axis=1).astype(F32) / 256.0
    onehot = (fitted_id[:, None] == jnp.arange(owners, dtype=jnp.int32)[None, :]).astype(jnp.int32)
    running = jnp.cumsum(onehot, axis=0)
    rank_in = jnp.sum(running * onehot, axis=1) - 1
    row_ids = fitted_id * (2 * capacity) + rank_in
    scaled = (route_weight[:, None] * out_grad.astype(F32)).astype(BF16)
    both_ids = jnp.concatenate([row_ids, row_ids + capacity])
    packer = (both_ids[None, :] == jnp.arange(owners * 2 * capacity, dtype=jnp.int32)[:, None]).astype(BF16)
    both = jnp.concatenate([tokens_x, scaled], axis=0)
    packed = jnp.dot(packer, both, preferred_element_type=F32).astype(BF16)
    packed = packed.reshape(owners, 2 * capacity, local_width)
    recv = lax.all_to_all(packed, ("y", "zh", "c"), split_axis=0, concat_axis=0, tiled=True)
    own = recv.transpose(1, 0, 2).reshape(2 * capacity, full_width)

    def swap_x(v, k):
        return lax.ppermute(v, "x", [(i, i ^ k) for i in range(nx)])

    w_own = jnp.concatenate([gate_w[0], up_w[0], down_w[0]], axis=0)
    w_others = [swap_x(w_own, k) for k in range(1, nx)]

    order = list(range(0, nz, 2)) + list(range(nz - 1, 0, -2))
    pairs = [(order[i], order[(i + 1) % nz]) for i in range(nz)]
    back = [(j, i) for i, j in pairs]

    def hop(v, way):
        return lax.ppermute(v, "zl", way)

    fore, aft = [own], [own]
    for _ in range(1, nz // 2):
        fore.append(hop(fore[-1], pairs))
        aft.append(hop(aft[-1], back))
    mid = full_width // 2
    far = [hop(fore[-1][:, :mid], pairs), hop(aft[-1][:, mid:], back)]
    parts, steps = [own], [0]
    for k in range(1, nz // 2):
        parts += [fore[k], aft[k]]
        steps += [k, nz - k]
    parts.append(jnp.concatenate(far, axis=1))
    steps.append(nz // 2)
    half = nz // 2

    def anchor(v):
        return v[:1, :1] * 0

    late = [anchor(parts[2]), anchor(parts[4])]
    weights = jnp.concatenate([w_own, w_others[0] + late[0], w_others[2], w_others[1] + late[1]], axis=0)

    group = nx * hid
    slots = nz * capacity
    place = jnp.where(zi % 2 == 0, zi // 2, nz - 1 - zi // 2)
    unit = jnp.arange(group, dtype=jnp.int32)
    offset = (unit // hid) ^ xi
    from_unit = (offset ^ (offset >> 1)) * hid + unit % hid
    unit_perm = (from_unit[:, None] == unit[None, :]).astype(BF16)
    column = jnp.arange(half * 2 * capacity, dtype=jnp.int32)
    lanes = 128
    rest = slots - lanes
    packed_col = jnp.arange((nx + 1) * lanes, dtype=jnp.int32)
    lane, part_of = packed_col % lanes, packed_col // lanes - 1
    slot = jnp.where(part_of < 0, lane, jnp.where(lane // rest == part_of, lanes + lane % rest, -2))

    sorted_f32 = 0.0
    x_half = []
    for h in range(2):
        rows = jnp.concatenate(parts[h * half : (h + 1) * half], axis=0)
        x_rows = rows.reshape(half, 2 * capacity, full_width)[:, :capacity]
        x_half.append(x_rows.reshape(half * capacity, full_width))
        pre = dot_nt(weights, rows).reshape(nx, 3 * hid, -1)
        gate_pre, up_pre = pre[:, :hid], pre[:, hid : 2 * hid]
        hidden_grad = jnp.roll(pre[:, 2 * hid :], -capacity, axis=2)
        gate_grad = (hidden_grad * up_pre * silu_slope(gate_pre)).astype(BF16).reshape(group, -1)
        went = jnp.repeat(jnp.array(steps[h * half : (h + 1) * half], jnp.int32), 2 * capacity)
        within = column % (2 * capacity)
        target = jnp.where(within < capacity, ((place - went + nz) % nz) * capacity + within, -1)
        slot_perm = (target[:, None] == slot[None, :]).astype(BF16)
        sorted_f32 = sorted_f32 + jnp.dot(gate_grad, slot_perm, preferred_element_type=F32)
    g_packed = jnp.dot(unit_perm, sorted_f32.astype(BF16), preferred_element_type=F32).astype(BF16)

    first = g_packed[:, :lanes]
    lasts = [g_packed[:, (1 + j) * lanes : (2 + j) * lanes] for j in range(nx)]
    tail = sum(v[j * hid : (j + 1) * hid] for j, v in enumerate(lasts))
    sent = jnp.concatenate([first, tail], axis=0)
    spread = jnp.broadcast_to(sent[None], (nz,) + sent.shape)
    spread = lax.all_to_all(spread, "zl", split_axis=0, concat_axis=0, tiled=True)
    later = (spread[0, :1, :1] * 0).reshape(1, 1)
    tails = spread[:, group:].reshape(nz * hid, lanes)
    cols = []
    for j in range(nx):
        theirs = spread[:, j * hid : (j + 1) * hid].reshape(nz * hid, lanes)
        both_j = jnp.concatenate([theirs, tails], axis=1)
        sums = dot_nt(jnp.concatenate([first, lasts[j]], axis=1), both_j) / float(slot_count)
        cols.append(sums.astype(BF16))
    part_sent = jnp.concatenate(cols, axis=1).reshape(nx, hid, nx * nz * hid)
    part = lax.all_to_all(part_sent, "x", split_axis=0, concat_axis=0, tiled=True)
    grad_rows = jnp.sum(part.astype(F32), axis=0)

    strip_width = full_width // (nx * nz)
    input_rows = 0.0
    for name, piece in zip(("xa", "xb"), x_half):
        own_piece = piece + (later if name == "xb" else anchor(sent))
        gathered = [own_piece] + [swap_x(piece, k) for k in range(1, nx)]
        rows = jnp.concatenate(gathered, axis=0)
        strip = lax.dynamic_slice_in_dim(rows, (xi * nz + zi) * strip_width, strip_width, 1)
        input_rows = input_rows + dot_tn(strip, rows) / float(slot_count)
    return (input_rows[None], grad_rows[None])


def solution(mesh):
    fine = Mesh(mesh.devices.reshape(4, 8, 4, 2, 2), ("x", "zl", "y", "zh", "c"))
    tok, exp = ("x", "zl"), ("y", "zh", "c")
    placed = (
        P(tok, exp),
        P(tok, exp),
        P(tok, None),
        P(tok, None),
        P(exp, tok, None),
        P(exp, tok, None),
        P(exp, tok, None),
    )
    return jax.shard_map(
        body,
        mesh=fine,
        in_specs=placed,
        out_specs=(P(exp, tok, None), P(exp, tok, None)),
        check_vma=False,
    )
```

```python
import jax
import jax.numpy as jnp
from jax import lax
from jax.sharding import Mesh, PartitionSpec as P


F32 = jnp.float32
BF16 = jnp.bfloat16


def silu_slope(values):
    sigma = jax.nn.sigmoid(values)
    return sigma * (1.0 + values * (1.0 - sigma))


def dot_nt(a, b):
    return lax.dot_general(a, b, (((1,), (1,)), ((), ())), preferred_element_type=F32)


def dot_tn(a, b):
    return lax.dot_general(a, b, (((0,), (0,)), ((), ())), preferred_element_type=F32)


def body(tokens_x, out_grad, expert_ids, route_q, gate_w, up_w, down_w):
    nx = lax.axis_size("x")
    nz = lax.axis_size("zl")
    owners = lax.axis_size("y") * lax.axis_size("zh") * lax.axis_size("c")
    xi = lax.axis_index("x")
    zi = lax.axis_index("zl")
    tok_rows, local_width = tokens_x.shape
    capacity = 2 * tok_rows // owners
    slot_count = capacity * nx * nz
    full_width = local_width * owners
    hid = gate_w.shape[1]

    fitted = expert_ids < owners
    fitted_id = jnp.sum(jnp.where(fitted, expert_ids, 0), axis=1)
    route_weight = jnp.sum(jnp.where(fitted, route_q, 0), axis=1).astype(F32) / 256.0
    onehot = (fitted_id[:, None] == jnp.arange(owners, dtype=jnp.int32)[None, :]).astype(jnp.int32)
    running = jnp.cumsum(onehot, axis=0)
    rank_in = jnp.sum(running * onehot, axis=1) - 1
    row_ids = fitted_id * (2 * capacity) + rank_in
    entries = jnp.concatenate([jnp.ones_like(route_weight), route_weight]).astype(BF16)
    both_ids = jnp.concatenate([row_ids, row_ids + capacity])
    row = jnp.arange(owners * 2 * capacity, dtype=jnp.int32)
    packer = jnp.where(both_ids[None, :] == row[:, None], entries[None, :], jnp.zeros((), BF16))
    both = jnp.concatenate([tokens_x, out_grad], axis=0)
    packed = jnp.dot(packer, both, preferred_element_type=F32).astype(BF16)
    packed = packed.reshape(owners, 2 * capacity, local_width)
    recv = lax.all_to_all(packed, ("y", "zh", "c"), split_axis=0, concat_axis=0, tiled=True)
    own = recv.transpose(1, 0, 2).reshape(2 * capacity, full_width)

    def swap_x(v, k):
        return lax.ppermute(v, "x", [(i, i ^ k) for i in range(nx)])

    w_own = jnp.concatenate([gate_w[0], up_w[0], down_w[0]], axis=0)
    w_others = [swap_x(w_own, k) for k in range(1, nx)]

    order = list(range(0, nz, 2)) + list(range(nz - 1, 0, -2))
    pairs = [(order[i], order[(i + 1) % nz]) for i in range(nz)]
    back = [(j, i) for i, j in pairs]

    def hop(v, way):
        return lax.ppermute(v, "zl", way)

    fore, aft = [own], [own]
    for _ in range(1, nz // 2):
        fore.append(hop(fore[-1], pairs))
        aft.append(hop(aft[-1], back))
    mid = full_width // 2
    far = [hop(fore[-1][:, :mid], pairs), hop(aft[-1][:, mid:], back)]
    parts, steps = [own], [0]
    for k in range(1, nz // 2):
        parts += [fore[k], aft[k]]
        steps += [k, nz - k]
    parts.append(jnp.concatenate(far, axis=1))
    steps.append(nz // 2)
    half = nz // 2

    def anchor(v):
        return v[:1, :1] * 0

    first = w_others[0] + anchor(parts[2])
    weights = jnp.concatenate([w_own, first, w_others[2], w_others[1]], axis=0)

    group = nx * hid
    slots = nz * capacity
    place = jnp.where(zi % 2 == 0, zi // 2, nz - 1 - zi // 2)
    unit = jnp.arange(group, dtype=jnp.int32)
    offset = (unit // hid) ^ xi
    from_unit = (offset ^ (offset >> 1)) * hid + unit % hid
    unit_perm = (from_unit[:, None] == unit[None, :]).astype(BF16)
    column = jnp.arange(half * 2 * capacity, dtype=jnp.int32)
    lanes = 128
    rest = slots - lanes
    packed_col = jnp.arange((nx + 1) * lanes, dtype=jnp.int32)
    lane, part_of = packed_col % lanes, packed_col // lanes - 1
    slot = jnp.where(part_of < 0, lane, jnp.where(lane // rest == part_of, lanes + lane % rest, -2))

    sorted_f32 = 0.0
    x_half = []
    for h in range(2):
        rows = jnp.concatenate(parts[h * half : (h + 1) * half], axis=0)
        x_rows = rows.reshape(half, 2 * capacity, full_width)[:, :capacity]
        x_half.append(x_rows.reshape(half * capacity, full_width))
        pre = dot_nt(weights, rows).reshape(nx, 3 * hid, -1)
        gate_pre, up_pre = pre[:, :hid], pre[:, hid : 2 * hid]
        hidden_grad = jnp.roll(pre[:, 2 * hid :], -capacity, axis=2)
        gate_grad = (hidden_grad * up_pre * silu_slope(gate_pre)).astype(BF16).reshape(group, -1)
        went = jnp.repeat(jnp.array(steps[h * half : (h + 1) * half], jnp.int32), 2 * capacity)
        within = column % (2 * capacity)
        target = jnp.where(within < capacity, ((place - went + nz) % nz) * capacity + within, -1)
        slot_perm = (target[:, None] == slot[None, :]).astype(BF16)
        sorted_f32 = sorted_f32 + jnp.dot(gate_grad, slot_perm, preferred_element_type=F32)
    g_packed = jnp.dot(unit_perm, sorted_f32.astype(BF16), preferred_element_type=F32).astype(BF16)

    first = g_packed[:, :lanes]
    lasts = [g_packed[:, (1 + j) * lanes : (2 + j) * lanes] for j in range(nx)]
    tail = sum(v[j * hid : (j + 1) * hid] for j, v in enumerate(lasts))
    sent = jnp.concatenate([first, tail], axis=0)
    spread = jnp.broadcast_to(sent[None], (nz,) + sent.shape)
    spread = lax.all_to_all(spread, "zl", split_axis=0, concat_axis=0, tiled=True)
    later = (spread[0, :1, :1] * 0).reshape(1, 1)
    tails = spread[:, group:].reshape(nz * hid, lanes)
    cols = []
    for j in range(nx):
        theirs = spread[:, j * hid : (j + 1) * hid].reshape(nz * hid, lanes)
        both_j = jnp.concatenate([theirs, tails], axis=1)
        sums = dot_nt(jnp.concatenate([first, lasts[j]], axis=1), both_j) / float(slot_count)
        cols.append(sums.astype(BF16))
    part_sent = jnp.concatenate(cols, axis=1).reshape(nx, hid, nx * nz * hid)
    part = lax.all_to_all(part_sent, "x", split_axis=0, concat_axis=0, tiled=True)
    grad_rows = jnp.sum(part.astype(F32), axis=0)

    strip_width = full_width // (nx * nz)
    input_rows = 0.0
    for name, piece in zip(("xa", "xb"), x_half):
        own_piece = piece + (later if name == "xb" else anchor(sent))
        gathered = [own_piece] + [swap_x(piece, k) for k in range(1, nx)]
        rows = jnp.concatenate(gathered, axis=0)
        strip = lax.dynamic_slice_in_dim(rows, (xi * nz + zi) * strip_width, strip_width, 1)
        input_rows = input_rows + dot_tn(strip, rows) / float(slot_count)
    return (input_rows[None], grad_rows[None])


def solution(mesh):
    fine = Mesh(mesh.devices.reshape(4, 8, 4, 2, 2), ("x", "zl", "y", "zh", "c"))
    tok, exp = ("x", "zl"), ("y", "zh", "c")
    placed = (
        P(tok, exp),
        P(tok, exp),
        P(tok, None),
        P(tok, None),
        P(exp, tok, None),
        P(exp, tok, None),
        P(exp, tok, None),
    )
    return jax.shard_map(
        body,
        mesh=fine,
        in_specs=placed,
        out_specs=(P(exp, tok, None), P(exp, tok, None)),
        check_vma=False,
    )
```

```python
import jax
import jax.numpy as jnp
from jax import lax
from jax.sharding import Mesh, PartitionSpec as P


F32 = jnp.float32
BF16 = jnp.bfloat16


def silu_slope(values):
    sigma = jax.nn.sigmoid(values)
    return sigma * (1.0 + values * (1.0 - sigma))


def dot_nt(a, b):
    return lax.dot_general(a, b, (((1,), (1,)), ((), ())), preferred_element_type=F32)


def dot_tn(a, b):
    return lax.dot_general(a, b, (((0,), (0,)), ((), ())), preferred_element_type=F32)


def body(tokens_x, out_grad, expert_ids, route_q, gate_w, up_w, down_w):
    nx = lax.axis_size("x")
    nz = lax.axis_size("zl")
    owners = lax.axis_size("y") * lax.axis_size("zh") * lax.axis_size("c")
    xi = lax.axis_index("x")
    zi = lax.axis_index("zl")
    tok_rows, local_width = tokens_x.shape
    capacity = 2 * tok_rows // owners
    slot_count = capacity * nx * nz
    full_width = local_width * owners
    hid = gate_w.shape[1]

    fitted = expert_ids < owners
    fitted_id = jnp.sum(jnp.where(fitted, expert_ids, 0), axis=1)
    route_weight = jnp.sum(jnp.where(fitted, route_q, 0), axis=1).astype(F32) / 256.0
    onehot = (fitted_id[:, None] == jnp.arange(owners, dtype=jnp.int32)[None, :]).astype(jnp.int32)
    running = jnp.cumsum(onehot, axis=0)
    rank_in = jnp.sum(running * onehot, axis=1) - 1
    row_ids = fitted_id * (2 * capacity) + rank_in
    entries = jnp.concatenate([jnp.ones_like(route_weight), route_weight]).astype(BF16)
    both_ids = jnp.concatenate([row_ids, row_ids + capacity])
    row = jnp.arange(owners * 2 * capacity, dtype=jnp.int32)
    packer = jnp.where(both_ids[None, :] == row[:, None], entries[None, :], jnp.zeros((), BF16))
    both = jnp.concatenate([tokens_x, out_grad], axis=0)
    packed = jnp.dot(packer, both, preferred_element_type=F32).astype(BF16)
    packed = packed.reshape(owners, 2 * capacity, local_width)
    recv = lax.all_to_all(packed, ("y", "zh", "c"), split_axis=0, concat_axis=0, tiled=True)
    own = recv.transpose(1, 0, 2).reshape(2 * capacity, full_width)

    def swap_x(v, k):
        return lax.ppermute(v, "x", [(i, i ^ k) for i in range(nx)])

    w_own = jnp.concatenate([gate_w[0], up_w[0], down_w[0]], axis=0)
    w_others = [swap_x(w_own, k) for k in range(1, nx)]

    order = list(range(0, nz, 2)) + list(range(nz - 1, 0, -2))
    pairs = [(order[i], order[(i + 1) % nz]) for i in range(nz)]
    back = [(j, i) for i, j in pairs]

    def hop(v, way):
        return lax.ppermute(v, "zl", way)

    fore, aft = [own], [own]
    for _ in range(1, nz // 2):
        fore.append(hop(fore[-1], pairs))
        aft.append(hop(aft[-1], back))
    mid = full_width // 2
    far = [hop(fore[-1][:, :mid], pairs), hop(aft[-1][:, mid:], back)]
    parts, steps = [own], [0]
    for k in range(1, nz // 2):
        parts += [fore[k], aft[k]]
        steps += [k, nz - k]
    parts.append(jnp.concatenate(far, axis=1))
    steps.append(nz // 2)
    cuts = (0, 5, nz)

    def anchor(v):
        return v[:1, :1] * 0

    first = w_others[0] + anchor(parts[2])
    weights = jnp.concatenate([w_own, first, w_others[2], w_others[1]], axis=0)

    group = nx * hid
    slots = nz * capacity
    place = jnp.where(zi % 2 == 0, zi // 2, nz - 1 - zi // 2)
    unit = jnp.arange(group, dtype=jnp.int32)
    offset = (unit // hid) ^ xi
    from_unit = (offset ^ (offset >> 1)) * hid + unit % hid
    unit_perm = (from_unit[:, None] == unit[None, :]).astype(BF16)
    lanes = 128
    rest = slots - lanes
    packed_col = jnp.arange((nx + 1) * lanes, dtype=jnp.int32)
    lane, part_of = packed_col % lanes, packed_col // lanes - 1
    slot = jnp.where(part_of < 0, lane, jnp.where(lane // rest == part_of, lanes + lane % rest, -2))

    sorted_f32 = 0.0
    x_half = []
    for h in range(2):
        count = cuts[h + 1] - cuts[h]
        rows = jnp.concatenate(parts[cuts[h] : cuts[h + 1]], axis=0)
        x_rows = rows.reshape(count, 2 * capacity, full_width)[:, :capacity]
        x_rows = x_rows.reshape(count * capacity, full_width)
        x_rows = jnp.pad(x_rows, ((0, -count * capacity % 8), (0, 0)))
        x_half.append(lax.optimization_barrier(x_rows))
        pre = dot_nt(weights, rows).reshape(nx, 3 * hid, -1)
        gate_pre, up_pre = pre[:, :hid], pre[:, hid : 2 * hid]
        hidden_grad = jnp.roll(pre[:, 2 * hid :], -capacity, axis=2)
        gate_grad = (hidden_grad * up_pre * silu_slope(gate_pre)).astype(BF16).reshape(group, -1)
        went = jnp.repeat(jnp.array(steps[cuts[h] : cuts[h + 1]], jnp.int32), 2 * capacity)
        within = jnp.arange(count * 2 * capacity, dtype=jnp.int32) % (2 * capacity)
        target = jnp.where(within < capacity, ((place - went + nz) % nz) * capacity + within, -1)
        slot_perm = (target[:, None] == slot[None, :]).astype(BF16)
        sorted_f32 = sorted_f32 + jnp.dot(gate_grad, slot_perm, preferred_element_type=F32)
    g_packed = jnp.dot(unit_perm, sorted_f32.astype(BF16), preferred_element_type=F32).astype(BF16)

    first = g_packed[:, :lanes]
    lasts = [g_packed[:, (1 + j) * lanes : (2 + j) * lanes] for j in range(nx)]
    tail = sum(v[j * hid : (j + 1) * hid] for j, v in enumerate(lasts))
    sent = jnp.concatenate([first, tail], axis=0)
    spread = jnp.broadcast_to(sent[None], (nz,) + sent.shape)
    spread = lax.all_to_all(spread, "zl", split_axis=0, concat_axis=0, tiled=True)
    later = (spread[0, :1, :1] * 0).reshape(1, 1)
    tails = spread[:, group:].reshape(nz * hid, lanes)
    cols = []
    for j in range(nx):
        theirs = spread[:, j * hid : (j + 1) * hid].reshape(nz * hid, lanes)
        both_j = jnp.concatenate([theirs, tails], axis=1)
        sums = dot_nt(jnp.concatenate([first, lasts[j]], axis=1), both_j) / float(slot_count)
        cols.append(sums.astype(BF16))
    part_sent = jnp.concatenate(cols, axis=1).reshape(nx, hid, nx * nz * hid)
    part = lax.all_to_all(part_sent, "x", split_axis=0, concat_axis=0, tiled=True)
    grad_rows = sum(part[j].astype(F32) for j in range(nx))

    strip_width = full_width // (nx * nz)
    input_rows = 0.0
    for name, piece in zip(("xa", "xb"), x_half):
        own_piece = piece + (later if name == "xb" else anchor(g_packed))
        gathered = [own_piece] + [swap_x(piece, k) for k in range(1, nx)]
        rows = jnp.concatenate(gathered, axis=0)
        strip = lax.dynamic_slice_in_dim(rows, (xi * nz + zi) * strip_width, strip_width, 1)
        input_rows = input_rows + dot_tn(strip, rows) / float(slot_count)
    return (input_rows[None], grad_rows[None])


def solution(mesh):
    fine = Mesh(mesh.devices.reshape(4, 8, 4, 2, 2), ("x", "zl", "y", "zh", "c"))
    tok, exp = ("x", "zl"), ("y", "zh", "c")
    placed = (
        P(tok, exp),
        P(tok, exp),
        P(tok, None),
        P(tok, None),
        P(exp, tok, None),
        P(exp, tok, None),
        P(exp, tok, None),
    )
    return jax.shard_map(
        body,
        mesh=fine,
        in_specs=placed,
        out_specs=(P(exp, tok, None), P(exp, tok, None)),
        check_vma=False,
    )
```
